32 devices in a mesh: groups: 2 (over y), lib: 4 (over z), tmpl: 2 (over x), sub: 2 (over core).
Axes of the slice: x: 2, y: 2, z: 4, core: 2. Of those that a mesh axis runs over, the one named last changes fastest.
Arguments:
- coords: float32 [512, 3, 128], P(('groups', 'lib', 'tmpl')), parts along dimension 0, may hold values from -5 to 5
- atom_type: int32 [512, 128], P(('groups', 'lib', 'tmpl')), parts along dimension 0, may hold values from 0 to 15
- channel: int32 [512, 128], P(('groups', 'lib', 'tmpl')), parts along dimension 0, may hold values from 0 to 2
- charge: float32 [512, 128], P(('groups', 'lib', 'tmpl')), parts along dimension 0, may hold values from -3 to 3
- pair_owner: int32 [512, 4], P(('groups', 'lib', 'tmpl')), parts along dimension 0, may hold values from 0 to 7, all different within a row; in each aligned block of 32 rows (0 to 31, 32 to 63, ...) at most 32 rows name the same one
- pair_slot: int32 [512, 4], P(('groups', 'lib', 'tmpl')), parts along dimension 0, may hold values from 0 to 511
- type_table: float32 [16, 2], replicated, may hold values from 0.3 to 3
- widths: float32 [5], replicated, may hold values from 0.3 to 1.2
- tmpl_points: float32 [4096, 3, 256], P(('lib', 'tmpl'), None, 'sub'), may hold values from -5 to 5
- tmpl_weights: bfloat16 [4096, 5, 256], P(('lib', 'tmpl'), None, 'sub'), may hold values from -3 to 3
Outputs:
- scores: float32 [512, 4], P(('groups', 'lib', 'tmpl')), parts along dimension 0
- pose_grad: float32 [512, 12], P(('groups', 'lib', 'tmpl')), parts along dimension 0
- weight_grad: float32 [8192, 5, 256], P(('groups', 'lib', 'tmpl'), None, 'sub'), parts along dimension 0
The draws below stay inside these ranges and needn't reach their ends.
There are 2 independent parts, one for each index of `groups`. The reference program is written for one: setup_inputs(seed, part) draws one part's arguments, and reference() takes and returns one part's arrays. A program takes and returns all parts, laid end to end along the dimension named above; an argument that names none is the same for every part. Nothing has to cross between parts.
Inputs may be any that keep to these rules, and one draw needn't show every extreme that they name: `pair_owner`: each row names 4 different owners; among the 32 rows of one device (aligned blocks) no owner is named more than 32 times, a bound that some block reaches.
All inputs are finite; a program needn't handle non-finite values.
Results may differ from the reference program's by a relative error of at most 0.0003.
Values sent between devices are 32-bit elements; how exact they have to be, the bound alone decides.
A program may use at most 64 MiB of HBM per device.

```python
import math
import jax
import jax.numpy as jnp
import numpy as np
from jax import lax

A = 128
TA = 256
F = 5
NT = 16
TOP = 4
TEMPLATES = 4096
CB = 32
OWNERS = 8
CAP = 32
TMPL_DEV = 512
BLOCKS = 256


def touch_ends(array, stream_key, least, largest):
    longest = array.shape.index(max(array.shape))
    spots = []
    for shift in (0, 1):
        where = [jax.random.randint(jax.random.fold_in(stream_key, axis), (), 0, length) for axis, length in enumerate(array.shape)]
        where[longest] = (where[longest] + shift) % array.shape[longest]
        spots.append(tuple(where))
    return array.at[spots[0]].set(least).at[spots[1]].set(largest)


def shard_levels(stream_key, dims, shards, low, largest):
    gain = 1.0
    for position, parts in shards:
        heights = jax.random.uniform(jax.random.fold_in(jax.random.fold_in(stream_key, 6), position), (parts,), jnp.float32, low / len(shards), largest / len(shards))
        gain = gain * jnp.repeat(jnp.exp(heights), dims[position] // parts).reshape((-1,) + (1,) * (len(dims) - 1 - position))
    return gain


def deal_out(stream_key, own, number, rows, amount, top, limit, slope):
    ranking = jax.random.permutation(stream_key, amount)
    crowded, ordinary = portions_of(amount, rows * top, limit, slope, True), portions_of(amount, rows * top, limit, slope, False)
    places = jnp.arange(amount)

    def named(tallies, rotation):
        used = int((tallies > 0).sum())
        fixed = max(1, used // 4)
        moved = fixed + (places - fixed + rotation * (used - fixed)) % max(1, amount - fixed)
        return jnp.zeros((amount,), jnp.int32).at[ranking[jnp.where(places < fixed, places, moved)]].set(jnp.asarray(tallies, jnp.int32))

    tallies = jnp.where(number % 4 == 0, named(crowded, number // 4), named(ordinary, number - number // 4 - 1))
    mixed = jax.random.permutation(jax.random.fold_in(own, 3), amount)
    giver, receiver = mixed[0:amount // 2 * 2:2], mixed[1:amount // 2 * 2:2]
    margin = jnp.minimum(tallies[giver] - 1, limit - tallies[receiver]) // 2
    margin = jnp.where((giver == ranking[0]) | (receiver == ranking[0]) | (tallies[receiver] == 0), 0, jnp.maximum(margin, 0))
    moved = jax.random.randint(jax.random.fold_in(own, 4), (amount // 2,), 0, 1 << 20) % (margin + 1)
    tallies = tallies.at[giver].add(-moved).at[receiver].add(moved)
    members = jnp.searchsorted(jnp.cumsum(tallies), jnp.arange(rows * top), side="right").astype(jnp.int32)
    listing = members.reshape(top, rows).T
    listing = listing[jax.random.permutation(jax.random.fold_in(own, 1), rows)]
    rotation = jax.random.randint(jax.random.fold_in(own, 2), (rows, 1), 0, top)
    return jnp.take_along_axis(listing, (jnp.arange(top)[None, :] + rotation) % top, axis=1)


def portions_of(amount, total, bound, lean, full):
    loads = [(1 << 20) // math.isqrt(standing ** lean) + 1 for standing in range(1, amount + 1)]
    largest = bound if full else min(bound, max(-(-total // amount), total * loads[0] // sum(loads)))
    least = 1 if total - largest >= amount - 1 else 0
    holding, spare = [largest] + [least] * (amount - 1), total - largest - least * (amount - 1)
    while spare > 0:
        free = [i for i in range(1, amount) if holding[i] < largest] or [i for i in range(1, amount) if holding[i] < bound]
        pool, remaining = sum([loads[i] for i in free]), spare
        for i in free:
            extra = min(bound - holding[i], max(1, remaining * loads[i] // pool), spare)
            holding[i] = holding[i] + extra
            spare = spare - extra
    return np.array(holding)


def centred(rng, shape, scale, limit, split=(), kind=jnp.bfloat16):
    array = jax.random.normal(rng, shape, jnp.float32) * scale
    if len(split) > 0:
        array = shard_levels(rng, shape, split, -0.22, 0.18) * array
    return jnp.clip(array, min=-limit, max=limit).astype(kind)


def setup_inputs(seed: int = 0, part: int = 0) -> dict:
    key_of = jax.random.split(jax.random.key(seed), 11)
    part_keys = jax.random.split(jax.random.fold_in(key_of[10], part), 11)
    coords = centred(part_keys[0], (BLOCKS, 3, A), 1.0, 5.0, ((0, 8),), jnp.float32)
    atom_type = touch_ends(jax.random.randint(part_keys[1], (BLOCKS, A), 0, NT), jax.random.fold_in(part_keys[1], 1), 0, NT - 1).astype(jnp.int32)
    channel = touch_ends(jax.random.randint(part_keys[2], (BLOCKS, A), 0, 3), jax.random.fold_in(part_keys[2], 1), 0, 2).astype(jnp.int32)
    charge = centred(part_keys[3], (BLOCKS, A), 0.5, 3.0, ((0, 8),), jnp.float32)
    pair_owner_keys = jax.random.split(jax.random.fold_in(part_keys[4], 1), BLOCKS // CB)
    pair_owner_turns = jax.random.permutation(jax.random.fold_in(part_keys[4], 3), BLOCKS // CB)
    pair_owner = jax.vmap(lambda own, number: deal_out(jax.random.fold_in(part_keys[4], 2), own, number, CB, OWNERS, TOP, CAP, 2))(pair_owner_keys, pair_owner_turns).reshape((BLOCKS, TOP))
    pair_slot = touch_ends(jax.random.randint(part_keys[5], (BLOCKS, TOP), 0, TMPL_DEV), jax.random.fold_in(part_keys[5], 1), 0, TMPL_DEV - 1).astype(jnp.int32)
    type_table = jnp.clip(jnp.exp(jax.random.uniform(key_of[6], (NT, 2), jnp.float32, math.log(0.3), math.log(3.0))), 0.3, 3.0)
    widths = jnp.clip(jnp.exp(jax.random.uniform(key_of[7], (F,), jnp.float32, math.log(0.3), math.log(1.2))), 0.3, 1.2)
    tmpl_points = centred(key_of[8], (TEMPLATES, 3, TA), 1.0, 5.0, ((0, 8), (2, 2)), jnp.float32)
    tmpl_weights = centred(key_of[9], (TEMPLATES, F, TA), 0.5, 3.0, ((0, 8), (2, 2)))
    return dict(coords=coords, atom_type=atom_type, channel=channel, charge=charge, pair_owner=pair_owner, pair_slot=pair_slot, type_table=type_table, widths=widths, tmpl_points=tmpl_points, tmpl_weights=tmpl_weights)


def atom_weights(atom_type, channel, charge, type_table):
    type_ids = jnp.arange(type_table.shape[0], dtype=jnp.int32)
    onehot = (atom_type[:, None, :] == type_ids[None, :, None]).astype(jnp.float32)
    steric = jnp.sum(onehot * type_table[None, :, 0:1], axis=1)
    strength = jnp.sum(onehot * type_table[None, :, 1:2], axis=1)
    channels = jnp.arange(3, dtype=jnp.int32)
    pharm_part = (channel[:, None, :] == channels[None, :, None]).astype(jnp.float32) * strength[:, None, :]
    return jnp.concatenate([steric[:, None, :], charge[:, None, :], pharm_part], axis=1)


def pair_terms(posed_xyz, atom_w, points, values, widths):
    offsets = posed_xyz[:, None, :] - points[:, :, None]
    sq_dist = jnp.sum(offsets * offsets, axis=0)
    kernel = jnp.exp(-widths[:, None, None] * sq_dist[None, :, :])
    crossed = kernel * atom_w[:, None, :]
    fields = crossed * values[:, :, None]
    intersection = jnp.sum(fields)
    scaled = jnp.sum(fields * (-2.0 * widths)[:, None, None], axis=0)
    forces = jnp.sum(scaled[None, :, :] * offsets, axis=1)
    shift_grad = jnp.sum(forces, axis=1)
    linear = jnp.sum(forces[:, None, :] * posed_xyz[None, :, :], axis=2).reshape(9)
    weight_part = jnp.sum(crossed, axis=2)
    return jnp.concatenate([intersection[None], shift_grad, linear]), weight_part


def reference(coords, atom_type, channel, charge, pair_owner, pair_slot, type_table, widths, tmpl_points, tmpl_weights):
    atom_w = atom_weights(atom_type, channel, charge, type_table)
    tmpl_w = tmpl_weights.astype(jnp.float32)
    templates = (pair_owner * TMPL_DEV + pair_slot).astype(jnp.int32)

    def advance(running, element):
        posed_xyz, block_w, tmpl_ids = element

        def single(tmpl_id):
            points = lax.dynamic_index_in_dim(tmpl_points, tmpl_id, 0, keepdims=False)
            values = lax.dynamic_index_in_dim(tmpl_w, tmpl_id, 0, keepdims=False)
            return pair_terms(posed_xyz, block_w, points, values, widths)

        results, weight_part = lax.map(single, tmpl_ids)
        running = running.at[tmpl_ids].add(weight_part)
        return running, results

    initial = jnp.zeros((TEMPLATES, F, TA), jnp.float32)
    weight_grad, results = lax.scan(advance, initial, (coords, atom_w, templates))
    scores = results[:, :, 0]
    pose_grad = jnp.sum(results[:, :, 1:], axis=1)
    return (scores, pose_grad, weight_grad)
```

```python
import functools
import math

import jax
import jax.numpy as jnp
from jax import lax
from jax.experimental import pallas as pl
from jax.experimental.pallas import tpu as pltpu
from jax.sharding import PartitionSpec as P

MESH = pl.DeviceIdType.MESH
F32 = jnp.float32
BF16 = jnp.bfloat16
ROWS = 16
MOMENTS = 10
SKEW = 2


def gather_kernel(libs, tmpls, xyz_ref, charge_ref, type_ref, chan_ref, owner_ref, slot_ref, real_ref, whole_ref, name_ref,
                  local_sem, z_send, z_recv, x_send, x_recv, s_send, s_recv):
    l = lax.axis_index("lib")
    t = lax.axis_index("tmpl")
    s = lax.axis_index("sub")
    half = real_ref.shape[3] // 2
    moves = [(xyz_ref, real_ref.at[l, t, pl.ds(0, 3)]), (charge_ref, real_ref.at[l, t, 3]), (type_ref, whole_ref.at[l, t, 0]),
             (chan_ref, whole_ref.at[l, t, 1]), (owner_ref, name_ref.at[l, t, 0]), (slot_ref, name_ref.at[l, t, 1])]
    moves = [pltpu.make_async_copy(src, dst, local_sem.at[n]) for n, (src, dst) in enumerate(moves)]
    for move in moves:
        move.start()
    barrier = pltpu.get_barrier_semaphore()

    @pl.loop(1, libs)
    def _(k):
        pl.semaphore_signal(barrier, inc=1, device_id={"lib": lax.rem(l + k, libs)}, device_id_type=MESH)

    @pl.loop(1, tmpls)
    def _(k):
        pl.semaphore_signal(barrier, inc=1, device_id={"tmpl": lax.rem(t + k, tmpls)}, device_id_type=MESH)

    pl.semaphore_signal(barrier, inc=1, device_id={"sub": 1 - s}, device_id_type=MESH)
    for move in moves:
        move.wait()
    pl.semaphore_wait(barrier, libs + tmpls - 1)

    def chunk(k, m):
        at = (lax.rem(l - k + libs, libs), lax.rem(t - m + tmpls, tmpls))
        part = pl.ds(s * half, half)
        return real_ref.at[at + (slice(None), part)], whole_ref.at[at + (slice(None), part)], name_ref.at[at + (s,)]

    class Bundle:
        def __init__(self, refs, send, recv, device):
            self.copies = [pltpu.make_async_remote_copy(
                src_ref=ref, dst_ref=ref, send_sem=send(n), recv_sem=recv(n), device_id=device, device_id_type=MESH)
                for n, ref in enumerate(refs)]

        def start(self):
            for c in self.copies:
                c.start()

        def wait_recv(self):
            for c in self.copies:
                c.wait_recv()

        def wait_send(self):
            for c in self.copies:
                c.wait_send()

    def z_copy(k):
        return Bundle(chunk(0, 0), lambda n: z_send.at[k, n], lambda n: z_recv.at[k, n], {"lib": lax.rem(l + k, libs)})

    def x_copy(k, m):
        return Bundle(chunk(k, 0), lambda n: x_send.at[k, m, n], lambda n: x_recv.at[k, m, n], {"tmpl": lax.rem(t + m, tmpls)})

    def s_copy(k, m):
        return Bundle(chunk(k, m), lambda n: s_send.at[k, m, n], lambda n: s_recv.at[k, m, n], {"sub": 1 - s})

    @pl.loop(1, tmpls)
    def _(m):
        x_copy(0, m).start()

    @pl.loop(1, libs)
    def _(k):
        z_copy(k).start()

    @pl.loop(1, libs)
    def _(k):
        z_copy(k).wait_recv()

        @pl.loop(1, tmpls)
        def _(m):
            x_copy(k, m).start()

        s_copy(k, 0).start()

    @pl.loop(1, tmpls)
    def _(m):
        @pl.loop(0, libs)
        def _(k):
            x_copy(k, m).wait_recv()
            s_copy(k, m).start()

    @pl.loop(1, libs)
    def _(k):
        z_copy(k).wait_send()
        s_copy(k, 0).wait_send()
        s_copy(k, 0).wait_recv()

    @pl.loop(1, tmpls)
    def _(m):
        @pl.loop(0, libs)
        def _(k):
            x_copy(k, m).wait_send()
            s_copy(k, m).wait_send()
            s_copy(k, m).wait_recv()


def gather_blocks(xyz, charge, types, chans, owners, slots, libs, tmpls):
    dma = pltpu.SemaphoreType.DMA
    blocks = charge.shape[0]
    lead = (libs, tmpls)
    vmem = pl.BlockSpec(memory_space=pltpu.VMEM)
    return pl.pallas_call(
        functools.partial(gather_kernel, libs, tmpls),
        out_shape=(jax.ShapeDtypeStruct(lead + (4, blocks, 128), F32), jax.ShapeDtypeStruct(lead + (2, blocks, 128), jnp.int32),
                   jax.ShapeDtypeStruct(lead + (2,) + owners.shape, jnp.int32)),
        in_specs=[pl.BlockSpec(memory_space=pl.ANY)] * 6,
        out_specs=(vmem,) * 3,
        scratch_shapes=[dma((6,)), dma((libs, 3)), dma((libs, 3)), dma(lead + (3,)), dma(lead + (3,)),
                        dma(lead + (3,)), dma(lead + (3,))],
        compiler_params=pltpu.CompilerParams(collective_id=0, has_side_effects=True, vmem_limit_bytes=60 << 20),
    )(xyz, charge, types, chans, owners, slots)


def split3(a):
    h = a.astype(BF16).astype(F32)
    r = a - h
    m = r.astype(BF16).astype(F32)
    return h, m, r - m


def split2(a):
    h = a.astype(BF16)
    return h, (a - h.astype(F32)).astype(BF16)


def slot_row(name_ref, dev, place):
    named = name_ref[dev, 0] == place
    return jnp.max(jnp.where(named, name_ref[dev, 1], -1), axis=0, keepdims=True)


class Pairs:
    def __init__(self, place, blocks, name_ref, widths_ref, table_ref, real_ref, whole_ref, points_ref, weights_ref, part_ref,
                 atom_ref, moment_ref, mask_ref, rows_ref, tmpl_ref, got_ref):
        self.place, self.blocks = place, blocks
        self.name_ref, self.widths_ref, self.table_ref = name_ref, widths_ref, table_ref
        self.real_ref, self.whole_ref, self.points_ref, self.weights_ref = real_ref, whole_ref, points_ref, weights_ref
        self.part_ref, self.atom_ref, self.moment_ref, self.mask_ref = part_ref, atom_ref, moment_ref, mask_ref
        self.rows_ref, self.tmpl_ref, self.got_ref = rows_ref, tmpl_ref, got_ref
        self.wide = [widths_ref[f] for f in range(5)]
        log2e = math.log2(math.e)
        self.scale = [-log2e * w for w in self.wide]
        self.ratio = self.wide[1] / self.wide[0]

    def plane(self, n):
        return pl.ds(n * self.blocks, self.blocks)

    def column(self, n, u, count=8):
        return pl.ds(n * self.blocks + u, count, stride=self.blocks)

    def clear(self):
        self.atom_ref[...] = jnp.zeros_like(self.atom_ref)
        self.moment_ref[...] = jnp.zeros_like(self.moment_ref)
        self.tmpl_ref[...] = jnp.zeros_like(self.tmpl_ref)

    def atoms(self, dev):
        x = [self.real_ref[dev, c] for c in range(3)]
        charge = self.real_ref[dev, 3]
        types = self.whole_ref[dev, 0]
        chan = self.whole_ref[dev, 1]
        steric = jnp.zeros(types.shape, F32)
        strength = jnp.zeros(types.shape, F32)
        for n in range(self.table_ref.shape[1]):
            same = types == n
            steric = jnp.where(same, self.table_ref[0, n], steric)
            strength = jnp.where(same, self.table_ref[1, n], strength)
        pharm = jnp.where(chan == 0, self.scale[2], jnp.where(chan == 1, self.scale[3], self.scale[4]))
        for c in range(3):
            self.mask_ref[self.plane(c)] = jnp.where(chan == c, 1.0, 0.0)
        second = [x[0] * x[0], x[0] * x[1], x[0] * x[2], x[1] * x[1], x[1] * x[2], x[2] * x[2]]
        norm = second[0] + second[3] + second[5]
        for s, scale in enumerate((self.scale[0], pharm)):
            for c, value in enumerate(x + [norm, None]):
                value = jnp.full(types.shape, scale) if value is None and s == 0 else scale if value is None else value * scale
                for p, piece in enumerate(split3(value)):
                    self.atom_ref[self.plane((3 * s + p) * 8 + c)] = piece
        for c, coef in enumerate((steric, charge, strength)):
            for k, moment in enumerate([None] + x + second):
                value = coef if moment is None else coef * moment
                high = value.astype(BF16).astype(F32)
                self.moment_ref[self.plane(2 * c * ROWS + k)] = high
                self.moment_ref[self.plane((2 * c + 1) * ROWS + k)] = value - high

    def templates(self, dev):
        slots = jnp.maximum(slot_row(self.name_ref, dev, self.place), 0)
        for u in range(self.blocks):
            there = pl.ds(slots[0, u], 1)
            for c in range(3):
                self.rows_ref[pl.ds(c * self.blocks + u, 1)] = self.points_ref[c, there, :]
            for f in range(5):
                self.rows_ref[pl.ds((3 + f) * self.blocks + u, 1)] = self.weights_ref[f, there, :]
        y = [self.rows_ref[self.plane(c)] for c in range(3)]
        norm = y[0] * y[0] + y[1] * y[1] + y[2] * y[2]
        for c, value in enumerate([-2.0 * y[0], -2.0 * y[1], -2.0 * y[2], jnp.ones_like(norm), norm]):
            for p, piece in enumerate(split3(value)):
                self.tmpl_ref[self.plane(8 * p + c)] = piece

    def front(self, u):
        def side(ref, base, order):
            pieces = [ref[self.column(base + 8 * p, u)] for p in range(3)]
            return jnp.concatenate([pieces[p] for p in order], axis=0).astype(BF16)

        xs = jnp.concatenate([side(self.atom_ref, 24 * s, (0, 0, 0, 1, 1, 2)) for s in range(2)], axis=1)
        ys = side(self.tmpl_ref, 0, (0, 1, 2, 0, 1, 0))
        return u, lax.dot_general(xs, ys, (((0,), (0,)), ((), ())), preferred_element_type=F32)

    def middle(self, u, dist):
        def side(c):
            rows = [self.moment_ref[self.column(2 * c * ROWS + 8 * r, u)] for r in range(4)]
            return jnp.concatenate(rows, axis=0).astype(BF16)

        def contract(power, lhs):
            hi, lo = split2(jnp.exp2(power))
            got = lax.dot_general(jnp.concatenate([lhs, lhs], axis=1), jnp.concatenate([hi, lo], axis=0),
                                  (((1,), (0,)), ((), ())), preferred_element_type=F32)
            return [got[r:r + ROWS] + got[r + ROWS:r + 2 * ROWS] for r in range(0, got.shape[0], 2 * ROWS)]

        strength = side(2)
        pharm = [strength * jnp.broadcast_to(self.mask_ref[pl.ds(c * self.blocks + u, 1)], strength.shape).astype(BF16)
                 for c in range(3)]
        near, far = dist[:128], dist[128:]
        return u, contract(near, side(0)) + contract(near * self.ratio, side(1)) + contract(far, jnp.concatenate(pharm, axis=0))

    def back(self, u, parts):
        for f, part in enumerate(parts):
            self.got_ref[self.column(f * ROWS, u)] = part[:8]
            self.got_ref[self.column(f * ROWS + 8, u, MOMENTS - 8)] = part[8:MOMENTS]

    def finish(self, dev):
        blocks = self.blocks
        lane = lax.broadcasted_iota(jnp.int32, (blocks, 128), 1)
        y = [self.rows_ref[self.plane(c)] for c in range(3)]
        score = jnp.zeros((blocks, 128), F32)
        total = [jnp.zeros((blocks, 128), F32)] * MOMENTS
        for f in range(5):
            v = self.rows_ref[self.plane(3 + f)]
            first = self.got_ref[self.plane(f * ROWS)]
            self.part_ref[f, pl.ds(dev * blocks, blocks)] = first
            score = score + v * first
            v = v * (-2.0 * self.wide[f])
            total = [t + v * (first if k == 0 else self.got_ref[self.plane(f * ROWS + k)]) for k, t in enumerate(total)]
        index = [[4, 5, 6], [5, 7, 8], [6, 8, 9]]
        values = [score] + [total[1 + c] - y[c] * total[0] for c in range(3)]
        values += [total[index[c][d]] - y[c] * total[1 + d] for c in range(3) for d in range(3)]
        packed = jnp.zeros((blocks, 128), F32)
        for q, value in enumerate(values):
            packed = jnp.where(lane == q, jnp.sum(value, axis=1, keepdims=True), packed)
        flat = jnp.concatenate([packed, jnp.zeros((128 - blocks, 128), F32)], axis=0).T[:16]
        valid = slot_row(self.name_ref, dev, self.place) >= 0
        valid = jnp.concatenate([jnp.where(valid, 1.0, 0.0), jnp.zeros((1, 128 - blocks), F32)], axis=1)
        flat = jnp.where(valid > 0.0, flat, 0.0)
        out = flat[0:4]
        for q in range(1, 4):
            out = out + pltpu.roll(flat[4 * q:4 * q + 4], 32 * q, 1)
        return out

    def chunk(self, dev):
        self.atoms(dev)
        self.templates(dev)
        fronts, middles = {}, {}
        for u in range(self.blocks + 2 * SKEW):
            if u < self.blocks:
                fronts[u] = self.front(u)
            if SKEW <= u < self.blocks + SKEW:
                middles[u - SKEW] = self.middle(*fronts.pop(u - SKEW))
            if u >= 2 * SKEW:
                self.back(*middles.pop(u - 2 * SKEW))
        return self.finish(dev)

    @staticmethod
    def scratch(blocks):
        return [pltpu.VMEM((n * blocks, 128), F32) for n in (48, 6 * ROWS, 3, 8, 24, 5 * ROWS)]


def pair_kernel(me, name_ref, widths_ref, table_ref, real_ref, whole_ref, points_ref, bf_weights_ref, part_ref, out_ref,
                weights_ref, *scratch):
    devices, _, blocks, _ = real_ref.shape
    pairs = Pairs(me(), blocks, name_ref, widths_ref, table_ref, real_ref, whole_ref, points_ref, weights_ref, part_ref, *scratch)
    pairs.clear()

    @pl.loop(0, 5)
    def _(f):
        weights_ref[f] = bf_weights_ref[f].astype(F32)

    @pl.loop(0, devices)
    def _(dev):
        out_ref[dev] = pairs.chunk(dev)


def run_pairs(me, names, widths, table, real, whole, points, weights):
    tmpl_count = points.shape[1]
    devices, _, blocks, _ = real.shape
    vmem = pl.BlockSpec(memory_space=pltpu.VMEM)
    smem = pl.BlockSpec(memory_space=pltpu.SMEM)
    return pl.pallas_call(
        functools.partial(pair_kernel, me),
        out_shape=(jax.ShapeDtypeStruct((5, devices * blocks, 128), F32), jax.ShapeDtypeStruct((devices, 4, 128), F32)),
        in_specs=[vmem, smem, smem, vmem, vmem, vmem, vmem],
        out_specs=(vmem, vmem),
        scratch_shapes=[pltpu.VMEM((5, tmpl_count, 128), F32)] + Pairs.scratch(blocks),
        compiler_params=pltpu.CompilerParams(vmem_limit_bytes=60 << 20),
    )(names, widths, table, real, whole, points, weights)


def return_kernel(libs, tmpls, res_ref, got_ref, local_sem, send_sem, recv_sem):
    l = lax.axis_index("lib")
    t = lax.axis_index("tmpl")
    s = lax.axis_index("sub")
    owners = libs * tmpls
    count = 2 * owners
    me = (l * tmpls + t) * 2 + s
    barrier = pltpu.get_barrier_semaphore()

    def peer(k):
        other = lax.rem(me + k, count)
        return other // 2, {"lib": other // (2 * tmpls), "tmpl": lax.rem(other // 2, tmpls), "sub": lax.rem(other, 2)}

    @pl.loop(1, count)
    def _(k):
        pl.semaphore_signal(barrier, inc=1, device_id=peer(k)[1], device_id_type=MESH)

    local = pltpu.make_async_copy(res_ref.at[l * tmpls + t], got_ref.at[me], local_sem)
    local.start()
    pl.semaphore_wait(barrier, count - 1)

    def copy(k):
        block, where = peer(k)
        return pltpu.make_async_remote_copy(
            src_ref=res_ref.at[block], dst_ref=got_ref.at[me], send_sem=send_sem.at[k], recv_sem=recv_sem.at[k],
            device_id=where, device_id_type=MESH)

    @pl.loop(1, count)
    def _(k):
        copy(k).start()

    local.wait()

    @pl.loop(1, count)
    def _(k):
        copy(k).wait()


def send_back(res, libs, tmpls):
    dma = pltpu.SemaphoreType.DMA
    count = 2 * libs * tmpls
    vmem = pl.BlockSpec(memory_space=pltpu.VMEM)
    return pl.pallas_call(
        functools.partial(return_kernel, libs, tmpls),
        out_shape=jax.ShapeDtypeStruct((count, 4, 128), F32),
        in_specs=[vmem],
        out_specs=vmem,
        scratch_shapes=[dma, dma((count,)), dma((count,))],
        compiler_params=pltpu.CompilerParams(collective_id=1, has_side_effects=True),
    )(res)


def last_kernel(me, got_ref, owner_ref, name_ref, part_ref, score_ref, pose_ref, wg_ref):
    per_block, blocks = owner_ref.shape
    devices = name_ref.shape[0]
    owner = owner_ref[...]
    place = me()

    def add(o, carry):
        total, scores = carry
        both = got_ref[2 * o] + got_ref[2 * o + 1]
        scores = jnp.where(owner == o, jnp.broadcast_to(both[0:1, :blocks], (per_block, blocks)), scores)
        return total + both, scores

    zeros = (jnp.zeros((4, 128), F32), jnp.zeros((per_block, blocks), F32))
    total, scores = lax.fori_loop(0, got_ref.shape[0] // 2, add, zeros)
    score_ref[...] = scores
    rows = [total] + [pltpu.roll(total, 128 - 32 * q, 1) for q in range(1, 4)]
    pose_ref[...] = jnp.concatenate([rows[0][1:4], rows[1], rows[2], rows[3][0:1]], axis=0)[:, :blocks]
    tmpl_count = wg_ref.shape[1]
    step = math.gcd(devices, 8)
    tile = math.gcd(tmpl_count, 256)
    count = step * blocks

    def spread(g):
        rows = []
        for n in range(step):
            row = slot_row(name_ref, g * step + n, place)
            rows.append(row)
        slots = jnp.concatenate(rows, axis=1)
        parts = [part_ref[f, pl.ds(g * count, count)] for f in range(5)]
        halves = [split2(p) for p in parts]
        rhs = jnp.concatenate([jnp.concatenate([h[n] for h in halves], axis=1) for n in range(2)], axis=0)
        for r in range(0, tmpl_count, tile):
            here = lax.broadcasted_iota(jnp.int32, (tile, count), 0) + r
            pick = jnp.where(here == slots, 1.0, 0.0).astype(BF16)
            out = lax.dot_general(jnp.concatenate([pick, pick], axis=1), rhs, (((1,), (0,)), ((), ())), preferred_element_type=F32)
            yield r, out

    for r, out in spread(0):
        for f in range(5):
            wg_ref[f, pl.ds(r, tile)] = out[:, 128 * f:128 * f + 128]

    if devices > step:
        @pl.loop(1, devices // step)
        def _(g):
            for r, out in spread(g):
                for f in range(5):
                    wg_ref[f, pl.ds(r, tile)] += out[:, 128 * f:128 * f + 128]


def last(me, got, owner_rows, names, parts, tmpl_count):
    per_block, blocks = owner_rows.shape
    vmem = pl.BlockSpec(memory_space=pltpu.VMEM)
    return pl.pallas_call(
        functools.partial(last_kernel, me),
        out_shape=(jax.ShapeDtypeStruct((per_block, blocks), F32), jax.ShapeDtypeStruct((12, blocks), F32),
                   jax.ShapeDtypeStruct((5, tmpl_count, 128), F32)),
        in_specs=[vmem] * 4,
        out_specs=(vmem,) * 3,
        compiler_params=pltpu.CompilerParams(vmem_limit_bytes=60 << 20),
    )(got, owner_rows, names, parts)


def local(libs, tmpls, coords, atom_type, channel, charge, pair_owner, pair_slot, type_table, widths, tmpl_points,
          tmpl_weights):
    owners, slots = pair_owner.T, pair_slot.T
    real, whole, names = gather_blocks(jnp.transpose(coords, (1, 0, 2)), charge, atom_type, channel, owners, slots, libs, tmpls)
    count = libs * tmpls
    real, whole, names = [a.reshape((count,) + a.shape[2:]) for a in (real, whole, names)]

    def me():
        return lax.axis_index("lib") * tmpls + lax.axis_index("tmpl")

    parts, res = run_pairs(me, names, widths, type_table.T, real, whole, jnp.transpose(tmpl_points, (1, 0, 2)),
                           jnp.transpose(tmpl_weights, (1, 0, 2)))
    got = send_back(res, libs, tmpls)
    scores, pose, weight_grad = last(me, got, owners, names, parts, tmpl_points.shape[0])
    return scores.T, pose.T, jnp.transpose(weight_grad, (1, 0, 2))


def solution(mesh):
    every = ("groups", "lib", "tmpl")
    in_specs = (P(every, None, None), P(every, None), P(every, None), P(every, None), P(every, None), P(every, None),
                P(), P(), P(("lib", "tmpl"), None, "sub"), P(("lib", "tmpl"), None, "sub"))
    out_specs = (P(every, None), P(every, None), P(every, None, "sub"))
    body = functools.partial(local, mesh.shape["lib"], mesh.shape["tmpl"])
    return jax.shard_map(body, mesh=mesh, in_specs=in_specs, out_specs=out_specs, check_vma=False)
```

```python
import functools
import math

import jax
import jax.numpy as jnp
from jax import lax
from jax.experimental import pallas as pl
from jax.experimental.pallas import tpu as pltpu
from jax.sharding import PartitionSpec as P

MESH = pl.DeviceIdType.MESH
F32 = jnp.float32
BF16 = jnp.bfloat16
ROWS = 16
MOMENTS = 10
LEAD = 2
LAG = 1


def split3(a):
    h = a.astype(BF16).astype(F32)
    r = a - h
    m = r.astype(BF16).astype(F32)
    return h, m, r - m


def split2(a):
    h = a.astype(BF16)
    return h, (a - h.astype(F32)).astype(BF16)


def slot_row(name_ref, dev, place):
    named = name_ref[dev, 0] == place
    return jnp.max(jnp.where(named, name_ref[dev, 1], -1), axis=0, keepdims=True)


class Pairs:
    def __init__(self, place, blocks, name_ref, widths_ref, table_ref, real_ref, whole_ref, points_ref, weights_ref, part_ref,
                 atom_ref, moment_ref, rows_ref, tmpl_ref, got_ref):
        self.place, self.blocks = place, blocks
        self.name_ref, self.widths_ref, self.table_ref = name_ref, widths_ref, table_ref
        self.real_ref, self.whole_ref, self.points_ref, self.weights_ref = real_ref, whole_ref, points_ref, weights_ref
        self.part_ref, self.atom_ref, self.moment_ref = part_ref, atom_ref, moment_ref
        self.rows_ref, self.tmpl_ref, self.got_ref = rows_ref, tmpl_ref, got_ref
        self.wide = [widths_ref[f] for f in range(5)]
        log2e = math.log2(math.e)
        self.scale = [-log2e * w for w in self.wide]
        self.ratio = self.wide[1] / self.wide[0]

    def plane(self, n):
        return pl.ds(n * (self.blocks + 1), self.blocks)

    def column(self, n, u, count=8):
        return pl.ds(n * (self.blocks + 1) + u, count, stride=self.blocks + 1)

    def clear(self):
        self.atom_ref[...] = jnp.zeros_like(self.atom_ref)
        self.moment_ref[...] = jnp.zeros_like(self.moment_ref)
        self.tmpl_ref[...] = jnp.zeros_like(self.tmpl_ref)

    def atoms(self, dev):
        x = [self.real_ref[dev, c] for c in range(3)]
        charge = self.real_ref[dev, 3]
        types = self.whole_ref[dev, 0]
        chan = self.whole_ref[dev, 1]
        steric = jnp.zeros(types.shape, F32)
        strength = jnp.zeros(types.shape, F32)
        for n in range(self.table_ref.shape[1]):
            same = types == n
            steric = jnp.where(same, self.table_ref[0, n], steric)
            strength = jnp.where(same, self.table_ref[1, n], strength)
        pharm = jnp.where(chan == 0, self.scale[2], jnp.where(chan == 1, self.scale[3], self.scale[4]))
        second = [x[0] * x[0], x[0] * x[1], x[0] * x[2], x[1] * x[1], x[1] * x[2], x[2] * x[2]]
        norm = second[0] + second[3] + second[5]
        for s, scale in enumerate((self.scale[0], pharm)):
            for c, value in enumerate(x + [norm, None]):
                value = jnp.full(types.shape, scale) if value is None and s == 0 else scale if value is None else value * scale
                for p, piece in enumerate(split3(value)):
                    self.atom_ref[self.plane((3 * s + p) * 8 + c)] = piece
        for c, coef in enumerate((steric, charge, strength)):
            for k, moment in enumerate([None] + x + second):
                value = coef if moment is None else coef * moment
                high = value.astype(BF16).astype(F32)
                low = value - high
                if c < 2:
                    self.moment_ref[self.plane(2 * c * ROWS + k)] = high
                    self.moment_ref[self.plane((2 * c + 1) * ROWS + k)] = low
                    continue
                for n in range(3):
                    self.moment_ref[self.plane(4 * ROWS + n * MOMENTS + k)] = jnp.where(chan == n, high, 0.0)
                    self.moment_ref[self.plane(6 * ROWS + n * MOMENTS + k)] = jnp.where(chan == n, low, 0.0)

    def templates(self, dev):
        slots = jnp.maximum(slot_row(self.name_ref, dev, self.place), 0)
        for u in range(self.blocks):
            there = pl.ds(slots[0, u], 1)
            for c in range(3):
                self.rows_ref[pl.ds(c * (self.blocks + 1) + u, 1)] = self.points_ref[c, there, :]
            for f in range(5):
                self.rows_ref[pl.ds((3 + f) * (self.blocks + 1) + u, 1)] = self.weights_ref[f, there, :]
        y = [self.rows_ref[self.plane(c)] for c in range(3)]
        norm = y[0] * y[0] + y[1] * y[1] + y[2] * y[2]
        for c, value in enumerate([-2.0 * y[0], -2.0 * y[1], -2.0 * y[2], jnp.ones_like(norm), norm]):
            for p, piece in enumerate(split3(value)):
                self.tmpl_ref[self.plane(8 * p + c)] = piece

    def front(self, u):
        def side(ref, base, order):
            pieces = [ref[self.column(base + 8 * p, u)] for p in range(3)]
            return jnp.concatenate([pieces[p] for p in order], axis=0).astype(BF16)

        xs = jnp.concatenate([side(self.atom_ref, 24 * s, (0, 0, 0, 1, 1, 2)) for s in range(2)], axis=1)
        ys = side(self.tmpl_ref, 0, (0, 1, 2, 0, 1, 0))
        return u, lax.dot_general(xs, ys, (((0,), (0,)), ((), ())), preferred_element_type=F32)

    def middle(self, both, e):
        base, rows = ((0, ROWS), (2 * ROWS, ROWS), (4 * ROWS, 2 * ROWS))[e]

        def side(u):
            parts = [self.moment_ref[self.column(base + r, u)] for r in range(0, 2 * rows, 8)]
            return jnp.concatenate(parts, axis=0).astype(BF16)

        powers = [d[128:] if e == 2 else d[:128] * self.ratio if e == 1 else d[:128] for _, d in both]
        lhs = jnp.concatenate([side(u) for u, _ in both], axis=0)
        rhs = jnp.concatenate([jnp.concatenate(split2(jnp.exp2(p)), axis=0) for p in powers], axis=1)
        got = lax.dot_general(jnp.concatenate([lhs, lhs], axis=1), rhs, (((1,), (0,)), ((), ())), preferred_element_type=F32)
        return [u for u, _ in both], base // 2, rows, got

    def back(self, us, base, rows, got):
        for n, u in enumerate(us):
            mine = got[2 * n * rows:(2 * n + 2) * rows, 128 * n:128 * n + 128]
            for r in range(0, rows, 8):
                self.got_ref[self.column(base + r, u)] = mine[r:r + 8] + mine[rows + r:rows + r + 8]

    def got(self, f, k):
        return self.got_ref[self.plane(f * ROWS + k if f < 2 else 2 * ROWS + (f - 2) * MOMENTS + k)]

    def finish(self, dev):
        blocks = self.blocks
        lane = lax.broadcasted_iota(jnp.int32, (blocks, 128), 1)
        y = [self.rows_ref[self.plane(c)] for c in range(3)]
        score = jnp.zeros((blocks, 128), F32)
        total = [jnp.zeros((blocks, 128), F32)] * MOMENTS
        for f in range(5):
            v = self.rows_ref[self.plane(3 + f)]
            first = self.got(f, 0)
            self.part_ref[f, pl.ds(dev * blocks, blocks)] = first
            score = score + v * first
            v = v * (-2.0 * self.wide[f])
            total = [t + v * (first if k == 0 else self.got(f, k)) for k, t in enumerate(total)]
        index = [[4, 5, 6], [5, 7, 8], [6, 8, 9]]
        values = [score] + [total[1 + c] - y[c] * total[0] for c in range(3)]
        values += [total[index[c][d]] - y[c] * total[1 + d] for c in range(3) for d in range(3)]
        packed = jnp.zeros((blocks, 128), F32)
        for q, value in enumerate(values):
            packed = jnp.where(lane == q, jnp.sum(value, axis=1, keepdims=True), packed)
        flat = jnp.concatenate([packed, jnp.zeros((128 - blocks, 128), F32)], axis=0).T[:16]
        valid = slot_row(self.name_ref, dev, self.place) >= 0
        valid = jnp.concatenate([jnp.where(valid, 1.0, 0.0), jnp.zeros((1, 128 - blocks), F32)], axis=1)
        flat = jnp.where(valid > 0.0, flat, 0.0)
        out = flat[0:4]
        for q in range(1, 4):
            out = out + pltpu.roll(flat[4 * q:4 * q + 4], 32 * q, 1)
        return out

    def chunk(self, dev):
        self.atoms(dev)
        self.templates(dev)
        groups = self.blocks // 2
        fronts, middles = {}, {}
        for n in range(3 * groups + LAG):
            g, e = divmod(n, 3)
            for ahead in range(0 if n == 0 else g + LEAD, g + LEAD + 1):
                if e == 0 and ahead < groups:
                    fronts[ahead] = [self.front(2 * ahead), self.front(2 * ahead + 1)]
            if g < groups:
                middles[n] = self.middle(fronts[g], e)
            if n >= LAG:
                self.back(*middles.pop(n - LAG))
        return self.finish(dev)

    @staticmethod
    def scratch(blocks):
        return [pltpu.VMEM((n * (blocks + 1), 128), F32) for n in (48, 8 * ROWS, 8, 24, 4 * ROWS)]


def main_kernel(libs, tmpls, xyz_ref, charge_ref, type_ref, chan_ref, owner_ref, slot_ref, points_hbm, weights_hbm, widths_ref,
                table_ref, part_ref, got_ref, name_ref, real_ref, whole_ref, res_ref, points_ref, bf_ref, weights_ref, local_sem,
                z_send, z_recv, x_send, x_recv, s_send, s_recv, r_send, r_recv, *scratch):
    l = lax.axis_index("lib")
    t = lax.axis_index("tmpl")
    s = lax.axis_index("sub")
    steps = libs * tmpls
    count = 2 * steps
    place = l * tmpls + t
    me = place * 2 + s
    blocks = real_ref.shape[2]
    half = blocks // 2
    moves = [(xyz_ref, real_ref.at[place, pl.ds(0, 3)]), (charge_ref, real_ref.at[place, 3]), (type_ref, whole_ref.at[place, 0]),
             (chan_ref, whole_ref.at[place, 1]), (owner_ref, name_ref.at[place, 0]), (slot_ref, name_ref.at[place, 1]),
             (points_hbm, points_ref), (weights_hbm, bf_ref)]
    moves = [pltpu.make_async_copy(src, dst, local_sem.at[n]) for n, (src, dst) in enumerate(moves)]
    for move in moves:
        move.start()
    barrier = pltpu.get_barrier_semaphore()

    @pl.loop(1, count)
    def _(k):
        other = lax.rem(me + k, count)
        where = {"lib": other // (2 * tmpls), "tmpl": lax.rem(other // 2, tmpls), "sub": lax.rem(other, 2)}
        pl.semaphore_signal(barrier, inc=1, device_id=where, device_id_type=MESH)

    for move in moves[:6]:
        move.wait()
    pl.semaphore_wait(barrier, count - 1)

    def owner_of(k, m):
        return lax.rem(l - k + libs, libs), lax.rem(t - m + tmpls, tmpls)

    def bundle(k, m, send, recv, device):
        lib, tmpl = owner_of(k, m)
        at = lib * tmpls + tmpl
        part = pl.ds(s * half, half)
        refs = (real_ref.at[at, :, part], whole_ref.at[at, :, part], name_ref.at[at, s])
        return [pltpu.make_async_remote_copy(src_ref=ref, dst_ref=ref, send_sem=send(n), recv_sem=recv(n), device_id=device,
                                             device_id_type=MESH) for n, ref in enumerate(refs)]

    def z_copy(k):
        return bundle(0, 0, lambda n: z_send.at[k, n], lambda n: z_recv.at[k, n], {"lib": lax.rem(l + k, libs)})

    def x_copy(k, m):
        return bundle(k, 0, lambda n: x_send.at[k, m, n], lambda n: x_recv.at[k, m, n], {"tmpl": lax.rem(t + m, tmpls)})

    def s_copy(k, m):
        return bundle(k, m, lambda n: s_send.at[k, m, n], lambda n: s_recv.at[k, m, n], {"sub": 1 - s})

    def back_copy(i, c):
        lib, tmpl = owner_of(i // tmpls, lax.rem(i, tmpls))
        where = {"lib": lib, "tmpl": tmpl, "sub": 1 - s} if c else {"lib": lib, "tmpl": tmpl}
        return pltpu.make_async_remote_copy(
            src_ref=res_ref.at[lib * tmpls + tmpl], dst_ref=got_ref.at[me], send_sem=r_send.at[i, c],
            recv_sem=r_recv.at[i, c], device_id=where, device_id_type=MESH)

    def all_of(copies, act):
        for c in copies:
            getattr(c, act)()

    def z_pump(k):
        all_of(z_copy(k), "wait_recv")

        @pl.loop(1, tmpls)
        def _(m):
            all_of(x_copy(k, m), "start")

        all_of(s_copy(k, 0), "start")

    def x_pump(k, m):
        all_of(x_copy(k, m), "wait_recv")
        all_of(s_copy(k, m), "start")

    @pl.loop(1, tmpls)
    def _(m):
        all_of(x_copy(0, m), "start")

    @pl.loop(1, libs)
    def _(k):
        all_of(z_copy(k), "start")

    pairs = Pairs(place, blocks, name_ref, widths_ref, table_ref, real_ref, whole_ref, points_ref, weights_ref, part_ref, *scratch)
    pairs.clear()
    for move in moves[6:]:
        move.wait()

    @pl.loop(0, 5)
    def _(f):
        weights_ref[f] = bf_ref[f].astype(F32)

    mine = pltpu.make_async_copy(res_ref.at[place], got_ref.at[me], local_sem.at[8])

    @pl.loop(0, steps)
    def _(i):
        k = i // tmpls
        m = lax.rem(i, tmpls)

        @pl.when((i > 0) & (m == 0) & (k + 1 < libs))
        def _():
            z_pump(k + 1)

        @pl.when((i > 0) & (m + 1 < tmpls))
        def _():
            x_pump(k, m + 1)

        @pl.when(i > 0)
        def _():
            all_of(s_copy(k, m), "wait_recv")

        @pl.when(i == 1)
        def _():
            mine.start()

        @pl.when(i > 0)
        def _():
            back_copy(i - 1, 1).start()

        @pl.when(i > 1)
        def _():
            back_copy(i - 1, 0).start()

        lib, tmpl = owner_of(k, m)
        dev = lib * tmpls + tmpl
        res_ref[dev] = pairs.chunk(dev)

        @pl.when(i == 0)
        def _():
            if tmpls > 1:
                x_pump(0, 1)
            if libs > 1:
                z_pump(1)

    mine.wait()

    @pl.loop(1, libs)
    def _(k):
        all_of(z_copy(k), "wait_send")
        all_of(s_copy(k, 0), "wait_send")

    @pl.loop(1, tmpls)
    def _(m):
        @pl.loop(0, libs)
        def _(k):
            all_of(x_copy(k, m), "wait_send")
            all_of(s_copy(k, m), "wait_send")

    back_copy(steps - 1, 1).start()
    back_copy(steps - 1, 0).start()
    back_copy(0, 1).wait()

    @pl.loop(1, steps)
    def _(i):
        for c in range(2):
            back_copy(i, c).wait()


def run(libs, tmpls, xyz, charge, types, chans, owners, slots, points, weights, widths, table):
    blocks = charge.shape[0]
    steps = libs * tmpls
    dma = pltpu.SemaphoreType.DMA
    vmem = pl.BlockSpec(memory_space=pltpu.VMEM)
    smem = pl.BlockSpec(memory_space=pltpu.SMEM)
    lead = (libs, tmpls)
    return pl.pallas_call(
        functools.partial(main_kernel, libs, tmpls),
        out_shape=(jax.ShapeDtypeStruct((5, steps * blocks, 128), F32), jax.ShapeDtypeStruct((2 * steps, 4, 128), F32),
                   jax.ShapeDtypeStruct((steps, 2) + owners.shape, jnp.int32)),
        in_specs=[pl.BlockSpec(memory_space=pl.ANY)] * 8 + [smem, smem],
        out_specs=(vmem,) * 3,
        scratch_shapes=[pltpu.VMEM((steps, 4, blocks, 128), F32), pltpu.VMEM((steps, 2, blocks, 128), jnp.int32),
                        pltpu.VMEM((steps, 4, 128), F32), pltpu.VMEM(points.shape, F32), pltpu.VMEM(weights.shape, BF16),
                        pltpu.VMEM(weights.shape, F32), dma((9,)), dma((libs, 3)), dma((libs, 3)), dma(lead + (3,)),
                        dma(lead + (3,)), dma(lead + (3,)), dma(lead + (3,)), dma((steps, 2)), dma((steps, 2))]
        + Pairs.scratch(blocks),
        compiler_params=pltpu.CompilerParams(collective_id=0, has_side_effects=True, vmem_limit_bytes=60 << 20),
    )(xyz, charge, types, chans, owners, slots, points, weights, widths, table)


def last_kernel(me, got_ref, owner_ref, name_ref, part_ref, score_ref, pose_ref, wg_ref):
    per_block, blocks = owner_ref.shape
    devices = name_ref.shape[0]
    owner = owner_ref[...]
    place = me()

    def add(o, carry):
        total, scores = carry
        both = got_ref[2 * o] + got_ref[2 * o + 1]
        scores = jnp.where(owner == o, jnp.broadcast_to(both[0:1, :blocks], (per_block, blocks)), scores)
        return total + both, scores

    zeros = (jnp.zeros((4, 128), F32), jnp.zeros((per_block, blocks), F32))
    total, scores = lax.fori_loop(0, got_ref.shape[0] // 2, add, zeros)
    score_ref[...] = scores
    rows = [total] + [pltpu.roll(total, 128 - 32 * q, 1) for q in range(1, 4)]
    pose_ref[...] = jnp.concatenate([rows[0][1:4], rows[1], rows[2], rows[3][0:1]], axis=0)[:, :blocks]
    tmpl_count = wg_ref.shape[1]
    step = math.gcd(devices, 8)
    tile = math.gcd(tmpl_count, 256)
    count = step * blocks

    def spread(g):
        rows = []
        for n in range(step):
            row = slot_row(name_ref, g * step + n, place)
            rows.append(row)
        slots = jnp.concatenate(rows, axis=1)
        parts = [part_ref[f, pl.ds(g * count, count)] for f in range(5)]
        halves = [split2(p) for p in parts]
        rhs = jnp.concatenate([jnp.concatenate([h[n] for h in halves], axis=1) for n in range(2)], axis=0)
        for r in range(0, tmpl_count, tile):
            here = lax.broadcasted_iota(jnp.int32, (tile, count), 0) + r
            pick = jnp.where(here == slots, 1.0, 0.0).astype(BF16)
            out = lax.dot_general(jnp.concatenate([pick, pick], axis=1), rhs, (((1,), (0,)), ((), ())), preferred_element_type=F32)
            yield r, out

    for r, out in spread(0):
        for f in range(5):
            wg_ref[f, pl.ds(r, tile)] = out[:, 128 * f:128 * f + 128]

    if devices > step:
        @pl.loop(1, devices // step)
        def _(g):
            for r, out in spread(g):
                for f in range(5):
                    wg_ref[f, pl.ds(r, tile)] += out[:, 128 * f:128 * f + 128]


def last(me, got, owner_rows, names, parts, tmpl_count):
    per_block, blocks = owner_rows.shape
    vmem = pl.BlockSpec(memory_space=pltpu.VMEM)
    return pl.pallas_call(
        functools.partial(last_kernel, me),
        out_shape=(jax.ShapeDtypeStruct((per_block, blocks), F32), jax.ShapeDtypeStruct((12, blocks), F32),
                   jax.ShapeDtypeStruct((5, tmpl_count, 128), F32)),
        in_specs=[vmem] * 4,
        out_specs=(vmem,) * 3,
        compiler_params=pltpu.CompilerParams(vmem_limit_bytes=60 << 20),
    )(got, owner_rows, names, parts)


def local(libs, tmpls, coords, atom_type, channel, charge, pair_owner, pair_slot, type_table, widths, tmpl_points,
          tmpl_weights):
    owners, slots = pair_owner.T, pair_slot.T

    def me():
        return lax.axis_index("lib") * tmpls + lax.axis_index("tmpl")

    parts, got, names = run(libs, tmpls, jnp.transpose(coords, (1, 0, 2)), charge, atom_type, channel, owners, slots,
                            jnp.transpose(tmpl_points, (1, 0, 2)), jnp.transpose(tmpl_weights, (1, 0, 2)), widths, type_table.T)
    scores, pose, weight_grad = last(me, got, owners, names, parts, tmpl_points.shape[0])
    return scores.T, pose.T, jnp.transpose(weight_grad, (1, 0, 2))


def solution(mesh):
    every = ("groups", "lib", "tmpl")
    in_specs = (P(every, None, None), P(every, None), P(every, None), P(every, None), P(every, None), P(every, None),
                P(), P(), P(("lib", "tmpl"), None, "sub"), P(("lib", "tmpl"), None, "sub"))
    out_specs = (P(every, None), P(every, None), P(every, None, "sub"))
    body = functools.partial(local, mesh.shape["lib"], mesh.shape["tmpl"])
    return jax.shard_map(body, mesh=mesh, in_specs=in_specs, out_specs=out_specs, check_vma=False)
```

```python
import functools
import math

import jax
import jax.numpy as jnp
from jax import lax
from jax.experimental import pallas as pl
from jax.experimental.pallas import tpu as pltpu
from jax.sharding import PartitionSpec as P

MESH = pl.DeviceIdType.MESH
F32 = jnp.float32
BF16 = jnp.bfloat16
ROWS = 16
MOMENTS = 10
LEAD = 10
LAG = 1


def split3(a):
    h = a.astype(BF16).astype(F32)
    r = a - h
    m = r.astype(BF16).astype(F32)
    return h, m, r - m


def split2(a):
    h = a.astype(BF16)
    return h, (a - h.astype(F32)).astype(BF16)


def slot_row(name_ref, dev, place):
    named = name_ref[dev, 0] == place
    return jnp.max(jnp.where(named, name_ref[dev, 1], -1), axis=0, keepdims=True)


class Pairs:
    def __init__(self, place, blocks, name_ref, widths_ref, table_ref, real_ref, whole_ref, points_ref, weights_ref, part_ref,
                 atom_ref, moment_ref, rows_ref, tmpl_ref, got_ref):
        self.place, self.blocks = place, blocks
        self.name_ref, self.widths_ref, self.table_ref = name_ref, widths_ref, table_ref
        self.real_ref, self.whole_ref, self.points_ref, self.weights_ref = real_ref, whole_ref, points_ref, weights_ref
        self.part_ref, self.atom_ref, self.moment_ref = part_ref, atom_ref, moment_ref
        self.rows_ref, self.tmpl_ref, self.got_ref = rows_ref, tmpl_ref, got_ref
        self.wide = [widths_ref[f] for f in range(5)]
        log2e = math.log2(math.e)
        self.scale = [-log2e * w for w in self.wide]
        self.ratio = self.wide[1] / self.wide[0]

    def plane(self, n):
        return pl.ds(n * (self.blocks + 1), self.blocks)

    def column(self, n, u, count=8):
        return pl.ds(n * (self.blocks + 1) + u, count, stride=self.blocks + 1)

    def clear(self):
        self.atom_ref[...] = jnp.zeros_like(self.atom_ref)
        self.moment_ref[...] = jnp.zeros_like(self.moment_ref)
        self.tmpl_ref[...] = jnp.zeros_like(self.tmpl_ref)

    def atoms(self, dev):
        x = [self.real_ref[dev, c] for c in range(3)]
        charge = self.real_ref[dev, 3]
        types = self.whole_ref[dev, 0]
        chan = self.whole_ref[dev, 1]
        steric = jnp.zeros(types.shape, F32)
        strength = jnp.zeros(types.shape, F32)
        for n in range(self.table_ref.shape[1]):
            same = types == n
            steric = jnp.where(same, self.table_ref[0, n], steric)
            strength = jnp.where(same, self.table_ref[1, n], strength)
        pharm = jnp.where(chan == 0, self.scale[2], jnp.where(chan == 1, self.scale[3], self.scale[4]))
        second = [x[0] * x[0], x[0] * x[1], x[0] * x[2], x[1] * x[1], x[1] * x[2], x[2] * x[2]]
        norm = second[0] + second[3] + second[5]
        for s, scale in enumerate((self.scale[0], pharm)):
            for c, value in enumerate(x + [norm, None]):
                value = jnp.full(types.shape, scale) if value is None and s == 0 else scale if value is None else value * scale
                for p, piece in enumerate(split3(value)):
                    self.atom_ref[self.plane((3 * s + p) * 8 + c)] = piece
        for c, coef in enumerate((steric, charge, strength)):
            for k, moment in enumerate([None] + x + second):
                value = coef if moment is None else coef * moment
                high = value.astype(BF16).astype(F32)
                low = value - high
                if c < 2:
                    self.moment_ref[self.plane(2 * c * ROWS + k)] = high
                    self.moment_ref[self.plane((2 * c + 1) * ROWS + k)] = low
                    continue
                for n in range(3):
                    self.moment_ref[self.plane(4 * ROWS + n * MOMENTS + k)] = jnp.where(chan == n, high, 0.0)
                    self.moment_ref[self.plane(6 * ROWS + n * MOMENTS + k)] = jnp.where(chan == n, low, 0.0)

    def templates(self, dev):
        slots = jnp.maximum(slot_row(self.name_ref, dev, self.place), 0)
        for u in range(self.blocks):
            there = pl.ds(slots[0, u], 1)
            for c in range(3):
                self.rows_ref[pl.ds(c * (self.blocks + 1) + u, 1)] = self.points_ref[c, there, :]
            for f in range(5):
                self.rows_ref[pl.ds((3 + f) * (self.blocks + 1) + u, 1)] = self.weights_ref[f, there, :]
        y = [self.rows_ref[self.plane(c)] for c in range(3)]
        norm = y[0] * y[0] + y[1] * y[1] + y[2] * y[2]
        for c, value in enumerate([-2.0 * y[0], -2.0 * y[1], -2.0 * y[2], jnp.ones_like(norm), norm]):
            for p, piece in enumerate(split3(value)):
                self.tmpl_ref[self.plane(8 * p + c)] = piece

    def front(self, u):
        def side(ref, base, order):
            pieces = [ref[self.column(base + 8 * p, u)] for p in range(3)]
            return jnp.concatenate([pieces[p] for p in order], axis=0).astype(BF16)

        xs = jnp.concatenate([side(self.atom_ref, 24 * s, (0, 0, 0, 1, 1, 2)) for s in range(2)], axis=1)
        ys = side(self.tmpl_ref, 0, (0, 1, 2, 0, 1, 0))
        return u, lax.dot_general(xs, ys, (((0,), (0,)), ((), ())), preferred_element_type=F32)

    def middle(self, u, dist, e):
        base, rows = ((0, ROWS), (2 * ROWS, ROWS), (4 * ROWS, 2 * ROWS))[e]
        power = dist[128:] if e == 2 else dist[:128] * self.ratio if e == 1 else dist[:128]
        lhs = jnp.concatenate([self.moment_ref[self.column(base + r, u)] for r in range(0, 2 * rows, 8)], axis=0).astype(BF16)
        rhs = jnp.concatenate(split2(jnp.exp2(power)), axis=1)
        got = lax.dot_general(lhs, rhs, (((1,), (0,)), ((), ())), preferred_element_type=F32)
        return u, base // 2, rows, got

    def back(self, u, base, rows, got):
        for r in range(0, rows, 8):
            mine = got[r:r + 8, :128] + got[r:r + 8, 128:] + got[rows + r:rows + r + 8, :128]
            self.got_ref[self.column(base + r, u)] = mine

    def got(self, f, k):
        return self.got_ref[self.plane(f * ROWS + k if f < 2 else 2 * ROWS + (f - 2) * MOMENTS + k)]

    def finish(self, dev):
        blocks = self.blocks
        lane = lax.broadcasted_iota(jnp.int32, (blocks, 128), 1)
        y = [self.rows_ref[self.plane(c)] for c in range(3)]
        score = jnp.zeros((blocks, 128), F32)
        total = [jnp.zeros((blocks, 128), F32)] * MOMENTS
        for f in range(5):
            v = self.rows_ref[self.plane(3 + f)]
            first = self.got(f, 0)
            self.part_ref[f, pl.ds(dev * blocks, blocks)] = first
            score = score + v * first
            v = v * (-2.0 * self.wide[f])
            total = [t + v * (first if k == 0 else self.got(f, k)) for k, t in enumerate(total)]
        index = [[4, 5, 6], [5, 7, 8], [6, 8, 9]]
        values = [score] + [total[1 + c] - y[c] * total[0] for c in range(3)]
        values += [total[index[c][d]] - y[c] * total[1 + d] for c in range(3) for d in range(3)]
        packed = jnp.zeros((blocks, 128), F32)
        for q, value in enumerate(values):
            packed = jnp.where(lane == q, jnp.sum(value, axis=1, keepdims=True), packed)
        flat = jnp.concatenate([packed, jnp.zeros((128 - blocks, 128), F32)], axis=0).T[:16]
        valid = slot_row(self.name_ref, dev, self.place) >= 0
        valid = jnp.concatenate([jnp.where(valid, 1.0, 0.0), jnp.zeros((1, 128 - blocks), F32)], axis=1)
        flat = jnp.where(valid > 0.0, flat, 0.0)
        out = flat[0:4]
        for q in range(1, 4):
            out = out + pltpu.roll(flat[4 * q:4 * q + 4], 32 * q, 1)
        return out

    def chunk(self, dev):
        self.atoms(dev)
        self.templates(dev)
        fronts, middles = {}, {}
        for n in range(-LEAD, 3 * self.blocks + LAG):
            u, e = divmod(n + LEAD, 3)
            if e == 0 and 0 <= u < self.blocks:
                fronts[u] = self.front(u)[1]
            u, e = divmod(n, 3)
            if 0 <= u < self.blocks:
                middles[n] = self.middle(u, fronts[u], e)
            if n >= LAG:
                self.back(*middles.pop(n - LAG))
        return self.finish(dev)

    @staticmethod
    def scratch(blocks):
        return [pltpu.VMEM((n * (blocks + 1), 128), F32) for n in (48, 8 * ROWS, 8, 24, 4 * ROWS)]


def main_kernel(libs, tmpls, xyz_ref, charge_ref, type_ref, chan_ref, owner_ref, slot_ref, points_hbm, weights_hbm, widths_ref,
                table_ref, part_ref, got_ref, name_ref, real_ref, whole_ref, res_ref, points_ref, bf_ref, weights_ref, local_sem,
                z_send, z_recv, x_send, x_recv, s_send, s_recv, r_send, r_recv, *scratch):
    l = lax.axis_index("lib")
    t = lax.axis_index("tmpl")
    s = lax.axis_index("sub")
    steps = libs * tmpls
    count = 2 * steps
    place = l * tmpls + t
    me = place * 2 + s
    blocks = real_ref.shape[2]
    half = blocks // 2
    moves = [(xyz_ref, real_ref.at[place, pl.ds(0, 3)]), (charge_ref, real_ref.at[place, 3]), (type_ref, whole_ref.at[place, 0]),
             (chan_ref, whole_ref.at[place, 1]), (owner_ref, name_ref.at[place, 0]), (slot_ref, name_ref.at[place, 1]),
             (points_hbm, points_ref), (weights_hbm, bf_ref)]
    moves = [pltpu.make_async_copy(src, dst, local_sem.at[n]) for n, (src, dst) in enumerate(moves)]
    for move in moves:
        move.start()
    barrier = pltpu.get_barrier_semaphore()

    @pl.loop(1, count)
    def _(k):
        other = lax.rem(me + k, count)
        where = {"lib": other // (2 * tmpls), "tmpl": lax.rem(other // 2, tmpls), "sub": lax.rem(other, 2)}
        pl.semaphore_signal(barrier, inc=1, device_id=where, device_id_type=MESH)

    for move in moves[:6]:
        move.wait()
    pl.semaphore_wait(barrier, count - 1)

    def lib_of(k, sign):
        if libs & (libs - 1):
            return lax.rem(l + sign * k + libs, libs)
        bits = [1 << b for b in range(libs.bit_length() - 1)]
        return sum((lax.rem(l // bit + k // bit, 2) * bit for bit in bits), jnp.int32(0))

    def owner_of(k, m):
        return lib_of(k, -1), lax.rem(t - m + tmpls, tmpls)

    def step_of(i):
        j = i // tmpls
        m = lax.rem(i, tmpls)
        return lib_step(j), m + ((j + 1) // libs) * (tmpls - 1 - 2 * m)

    def lib_step(j):
        return (lax.rem(j, max(libs - 1, 1)) + 1) * ((j + libs - 1) // libs)

    def bundle(k, m, send, recv, device):
        lib, tmpl = owner_of(k, m)
        at = lib * tmpls + tmpl
        part = pl.ds(s * half, half)
        refs = (real_ref.at[at, :, part], whole_ref.at[at, :, part], name_ref.at[at, s])
        return [pltpu.make_async_remote_copy(src_ref=ref, dst_ref=ref, send_sem=send(n), recv_sem=recv(n), device_id=device,
                                             device_id_type=MESH) for n, ref in enumerate(refs)]

    def z_copy(k):
        return bundle(0, 0, lambda n: z_send.at[k, n], lambda n: z_recv.at[k, n], {"lib": lib_of(k, 1)})

    def x_copy(k, m):
        return bundle(k, 0, lambda n: x_send.at[k, m, n], lambda n: x_recv.at[k, m, n], {"tmpl": lax.rem(t + m, tmpls)})

    def s_copy(k, m):
        return bundle(k, m, lambda n: s_send.at[k, m, n], lambda n: s_recv.at[k, m, n], {"sub": 1 - s})

    def back_copy(i, c):
        lib, tmpl = owner_of(*step_of(i))
        where = {"lib": lib, "tmpl": tmpl, "sub": 1 - s} if c else {"lib": lib, "tmpl": tmpl}
        return pltpu.make_async_remote_copy(
            src_ref=res_ref.at[lib * tmpls + tmpl], dst_ref=got_ref.at[me], send_sem=r_send.at[i, c],
            recv_sem=r_recv.at[i, c], device_id=where, device_id_type=MESH)

    def all_of(copies, act):
        for c in copies:
            getattr(c, act)()

    def z_pump(k):
        all_of(z_copy(k), "wait_recv")

        @pl.loop(1, tmpls)
        def _(m):
            all_of(x_copy(k, m), "start")

        all_of(s_copy(k, 0), "start")

    def x_pump(k, m):
        all_of(x_copy(k, m), "wait_recv")
        all_of(s_copy(k, m), "start")

    @pl.loop(1, tmpls)
    def _(m):
        all_of(x_copy(0, m), "start")

    @pl.loop(1, libs)
    def _(j):
        all_of(z_copy(lib_step(j)), "start")

    pairs = Pairs(place, blocks, name_ref, widths_ref, table_ref, real_ref, whole_ref, points_ref, weights_ref, part_ref, *scratch)
    pairs.clear()
    for move in moves[6:]:
        move.wait()

    @pl.loop(0, 5)
    def _(f):
        weights_ref[f] = bf_ref[f].astype(F32)

    mine = pltpu.make_async_copy(res_ref.at[place], got_ref.at[me], local_sem.at[8])

    @pl.loop(0, steps)
    def _(i):
        k, m = step_of(i)
        j = i // tmpls
        k1, m1 = step_of(i + 1)

        @pl.when((i > 0) & (lax.rem(i, tmpls) == 0) & (j + 1 < libs))
        def _():
            z_pump(lib_step(j + 1))

        @pl.when((i > 0) & (i + 1 < steps) & (m1 > 0))
        def _():
            x_pump(k1, m1)

        @pl.when(i > 0)
        def _():
            all_of(s_copy(k, m), "wait_recv")

        @pl.when(i == 1)
        def _():
            mine.start()

        @pl.when(i > 0)
        def _():
            back_copy(i - 1, 1).start()

        @pl.when(i > 1)
        def _():
            back_copy(i - 1, 0).start()

        lib, tmpl = owner_of(k, m)
        dev = lib * tmpls + tmpl
        res_ref[dev] = pairs.chunk(dev)

        @pl.when(i == 0)
        def _():
            if tmpls > 1:
                x_pump(0, 1)
            if libs > 1:
                z_pump(lib_step(1))

    mine.wait()

    @pl.loop(1, libs)
    def _(k):
        all_of(z_copy(k), "wait_send")
        all_of(s_copy(k, 0), "wait_send")

    @pl.loop(1, tmpls)
    def _(m):
        @pl.loop(0, libs)
        def _(k):
            all_of(x_copy(k, m), "wait_send")
            all_of(s_copy(k, m), "wait_send")

    back_copy(steps - 1, 1).start()
    back_copy(steps - 1, 0).start()
    back_copy(0, 1).wait()

    @pl.loop(1, steps)
    def _(i):
        for c in range(2):
            back_copy(i, c).wait()


def run(libs, tmpls, xyz, charge, types, chans, owners, slots, points, weights, widths, table):
    blocks = charge.shape[0]
    steps = libs * tmpls
    dma = pltpu.SemaphoreType.DMA
    vmem = pl.BlockSpec(memory_space=pltpu.VMEM)
    smem = pl.BlockSpec(memory_space=pltpu.SMEM)
    lead = (libs, tmpls)
    return pl.pallas_call(
        functools.partial(main_kernel, libs, tmpls),
        out_shape=(jax.ShapeDtypeStruct((5, steps * blocks, 128), F32), jax.ShapeDtypeStruct((2 * steps, 4, 128), F32),
                   jax.ShapeDtypeStruct((steps, 2) + owners.shape, jnp.int32)),
        in_specs=[pl.BlockSpec(memory_space=pl.ANY)] * 8 + [smem, smem],
        out_specs=(vmem,) * 3,
        scratch_shapes=[pltpu.VMEM((steps, 4, blocks, 128), F32), pltpu.VMEM((steps, 2, blocks, 128), jnp.int32),
                        pltpu.VMEM((steps, 4, 128), F32), pltpu.VMEM(points.shape, F32), pltpu.VMEM(weights.shape, BF16),
                        pltpu.VMEM(weights.shape, F32), dma((9,)), dma((libs, 3)), dma((libs, 3)), dma(lead + (3,)),
                        dma(lead + (3,)), dma(lead + (3,)), dma(lead + (3,)), dma((steps, 2)), dma((steps, 2))]
        + Pairs.scratch(blocks),
        compiler_params=pltpu.CompilerParams(collective_id=0, has_side_effects=True, vmem_limit_bytes=60 << 20),
    )(xyz, charge, types, chans, owners, slots, points, weights, widths, table)


def last_kernel(me, got_ref, owner_ref, name_ref, part_ref, score_ref, pose_ref, wg_ref):
    per_block, blocks = owner_ref.shape
    devices = name_ref.shape[0]
    owner = owner_ref[...]
    place = me()

    def add(o, carry):
        total, scores = carry
        both = got_ref[2 * o] + got_ref[2 * o + 1]
        scores = jnp.where(owner == o, jnp.broadcast_to(both[0:1, :blocks], (per_block, blocks)), scores)
        return total + both, scores

    zeros = (jnp.zeros((4, 128), F32), jnp.zeros((per_block, blocks), F32))
    total, scores = lax.fori_loop(0, got_ref.shape[0] // 2, add, zeros)
    score_ref[...] = scores
    rows = [total] + [pltpu.roll(total, 128 - 32 * q, 1) for q in range(1, 4)]
    pose_ref[...] = jnp.concatenate([rows[0][1:4], rows[1], rows[2], rows[3][0:1]], axis=0)[:, :blocks]
    tmpl_count = wg_ref.shape[1]
    step = math.gcd(devices, 8)
    tile = math.gcd(tmpl_count, 256)
    count = step * blocks

    def spread(g):
        rows = []
        for n in range(step):
            row = slot_row(name_ref, g * step + n, place)
            rows.append(row)
        slots = jnp.concatenate(rows, axis=1)
        parts = [part_ref[f, pl.ds(g * count, count)] for f in range(5)]
        halves = [split2(p) for p in parts]
        rhs = jnp.concatenate([jnp.concatenate([h[n] for h in halves], axis=1) for n in range(2)], axis=0)
        for r in range(0, tmpl_count, tile):
            here = lax.broadcasted_iota(jnp.int32, (tile, count), 0) + r
            pick = jnp.where(here == slots, 1.0, 0.0).astype(BF16)
            out = lax.dot_general(jnp.concatenate([pick, pick], axis=1), rhs, (((1,), (0,)), ((), ())), preferred_element_type=F32)
            yield r, out

    for r, out in spread(0):
        for f in range(5):
            wg_ref[f, pl.ds(r, tile)] = out[:, 128 * f:128 * f + 128]

    if devices > step:
        @pl.loop(1, devices // step)
        def _(g):
            for r, out in spread(g):
                for f in range(5):
                    wg_ref[f, pl.ds(r, tile)] += out[:, 128 * f:128 * f + 128]


def last(me, got, owner_rows, names, parts, tmpl_count):
    per_block, blocks = owner_rows.shape
    vmem = pl.BlockSpec(memory_space=pltpu.VMEM)
    return pl.pallas_call(
        functools.partial(last_kernel, me),
        out_shape=(jax.ShapeDtypeStruct((per_block, blocks), F32), jax.ShapeDtypeStruct((12, blocks), F32),
                   jax.ShapeDtypeStruct((5, tmpl_count, 128), F32)),
        in_specs=[vmem] * 4,
        out_specs=(vmem,) * 3,
        compiler_params=pltpu.CompilerParams(vmem_limit_bytes=60 << 20),
    )(got, owner_rows, names, parts)


def local(libs, tmpls, coords, atom_type, channel, charge, pair_owner, pair_slot, type_table, widths, tmpl_points,
          tmpl_weights):
    owners, slots = pair_owner.T, pair_slot.T

    def me():
        return lax.axis_index("lib") * tmpls + lax.axis_index("tmpl")

    parts, got, names = run(libs, tmpls, jnp.transpose(coords, (1, 0, 2)), charge, atom_type, channel, owners, slots,
                            jnp.transpose(tmpl_points, (1, 0, 2)), jnp.transpose(tmpl_weights, (1, 0, 2)), widths, type_table.T)
    scores, pose, weight_grad = last(me, got, owners, names, parts, tmpl_points.shape[0])
    return scores.T, pose.T, jnp.transpose(weight_grad, (1, 0, 2))


def solution(mesh):
    every = ("groups", "lib", "tmpl")
    in_specs = (P(every, None, None), P(every, None), P(every, None), P(every, None), P(every, None), P(every, None),
                P(), P(), P(("lib", "tmpl"), None, "sub"), P(("lib", "tmpl"), None, "sub"))
    out_specs = (P(every, None), P(every, None), P(every, None, "sub"))
    body = functools.partial(local, mesh.shape["lib"], mesh.shape["tmpl"])
    return jax.shard_map(body, mesh=mesh, in_specs=in_specs, out_specs=out_specs, check_vma=False)
```

```python
import functools
import math

import jax
import jax.numpy as jnp
from jax import lax
from jax.experimental import pallas as pl
from jax.experimental.pallas import tpu as pltpu
from jax.sharding import PartitionSpec as P

MESH = pl.DeviceIdType.MESH
F32 = jnp.float32
BF16 = jnp.bfloat16
ROWS = 16
MOMENTS = 10
LEAD = 10
LAG = 1


def split3(a):
    h = a.astype(BF16).astype(F32)
    r = a - h
    m = r.astype(BF16).astype(F32)
    return h, m, r - m


def split2(a):
    h = a.astype(BF16)
    return h, (a - h.astype(F32)).astype(BF16)


def slot_row(name_ref, dev, place):
    named = name_ref[dev, 0] == place
    return jnp.max(jnp.where(named, name_ref[dev, 1], -1), axis=0, keepdims=True)


class Pairs:
    def __init__(self, place, blocks, name_ref, widths_ref, table_ref, real_ref, whole_ref, points_ref, weights_ref, part_ref,
                 atom_ref, moment_ref, rows_ref, tmpl_ref, got_ref):
        self.place, self.blocks = place, blocks
        self.name_ref, self.widths_ref, self.table_ref = name_ref, widths_ref, table_ref
        self.real_ref, self.whole_ref, self.points_ref, self.weights_ref = real_ref, whole_ref, points_ref, weights_ref
        self.part_ref, self.atom_ref, self.moment_ref = part_ref, atom_ref, moment_ref
        self.rows_ref, self.tmpl_ref, self.got_ref = rows_ref, tmpl_ref, got_ref
        self.wide = [widths_ref[f] for f in range(5)]
        log2e = math.log2(math.e)
        self.scale = [-log2e * w for w in self.wide]
        self.ratio = self.wide[1] / self.wide[0]

    def plane(self, n):
        return pl.ds(n * (self.blocks + 1), self.blocks)

    def column(self, n, u, count=8):
        return pl.ds(n * (self.blocks + 1) + u, count, stride=self.blocks + 1)

    def clear(self):
        self.atom_ref[...] = jnp.zeros_like(self.atom_ref)
        self.moment_ref[...] = jnp.zeros_like(self.moment_ref)
        self.tmpl_ref[...] = jnp.zeros_like(self.tmpl_ref)

    def atoms(self, dev):
        x = [self.real_ref[dev, c] for c in range(3)]
        charge = self.real_ref[dev, 3]
        types = self.whole_ref[dev, 0]
        chan = self.whole_ref[dev, 1]
        steric = jnp.zeros(types.shape, F32)
        strength = jnp.zeros(types.shape, F32)
        for n in range(self.table_ref.shape[1]):
            same = types == n
            steric = jnp.where(same, self.table_ref[0, n], steric)
            strength = jnp.where(same, self.table_ref[1, n], strength)
        pharm = jnp.where(chan == 0, self.scale[2], jnp.where(chan == 1, self.scale[3], self.scale[4]))
        second = [x[0] * x[0], x[0] * x[1], x[0] * x[2], x[1] * x[1], x[1] * x[2], x[2] * x[2]]
        norm = second[0] + second[3] + second[5]
        for s, scale in enumerate((self.scale[0], pharm)):
            for c, value in enumerate(x + [norm, None]):
                value = jnp.full(types.shape, scale) if value is None and s == 0 else scale if value is None else value * scale
                for p, piece in enumerate(split3(value)):
                    self.atom_ref[self.plane((3 * s + p) * 8 + c)] = piece
        for c, coef in enumerate((steric, charge, strength)):
            for k, moment in enumerate([None] + x + second):
                value = coef if moment is None else coef * moment
                high = value.astype(BF16).astype(F32)
                low = value - high
                if c < 2:
                    self.moment_ref[self.plane(2 * c * ROWS + k)] = high
                    self.moment_ref[self.plane((2 * c + 1) * ROWS + k)] = low
                    continue
                for n in range(3):
                    self.moment_ref[self.plane(4 * ROWS + n * MOMENTS + k)] = jnp.where(chan == n, high, 0.0)
                    self.moment_ref[self.plane(6 * ROWS + n * MOMENTS + k)] = jnp.where(chan == n, low, 0.0)

    def templates(self, dev):
        slots = jnp.maximum(slot_row(self.name_ref, dev, self.place), 0)
        for u in range(self.blocks):
            there = pl.ds(slots[0, u], 1)
            for c in range(3):
                self.rows_ref[pl.ds(c * (self.blocks + 1) + u, 1)] = self.points_ref[c, there, :]
            for f in range(5):
                self.rows_ref[pl.ds((3 + f) * (self.blocks + 1) + u, 1)] = self.weights_ref[f, there, :]
        y = [self.rows_ref[self.plane(c)] for c in range(3)]
        norm = y[0] * y[0] + y[1] * y[1] + y[2] * y[2]
        for c, value in enumerate([-2.0 * y[0], -2.0 * y[1], -2.0 * y[2], jnp.ones_like(norm), norm]):
            for p, piece in enumerate(split3(value)):
                self.tmpl_ref[self.plane(8 * p + c)] = piece

    def front(self, u):
        def side(ref, base, order):
            pieces = [ref[self.column(base + 8 * p, u)] for p in range(3)]
            return jnp.concatenate([pieces[p] for p in order], axis=0).astype(BF16)

        xs = jnp.concatenate([side(self.atom_ref, 24 * s, (0, 0, 0, 1, 1, 2)) for s in range(2)], axis=1)
        ys = side(self.tmpl_ref, 0, (0, 1, 2, 0, 1, 0))
        return u, lax.dot_general(xs, ys, (((0,), (0,)), ((), ())), preferred_element_type=F32)

    def middle(self, u, dist, e):
        base, rows = ((0, ROWS), (2 * ROWS, ROWS), (4 * ROWS, 2 * ROWS))[e]
        power = dist[128:] if e == 2 else dist[:128] * self.ratio if e == 1 else dist[:128]
        lhs = jnp.concatenate([self.moment_ref[self.column(base + r, u)] for r in range(0, 2 * rows, 8)], axis=0).astype(BF16)
        rhs = jnp.concatenate(split2(jnp.exp2(power)), axis=1)
        got = lax.dot_general(lhs, rhs, (((1,), (0,)), ((), ())), preferred_element_type=F32)
        return u, base // 2, rows, got

    def back(self, u, base, rows, got):
        for r in range(0, rows, 8):
            mine = got[r:r + 8, :128] + got[r:r + 8, 128:] + got[rows + r:rows + r + 8, :128]
            self.got_ref[self.column(base + r, u)] = mine

    def got(self, f, k):
        return self.got_ref[self.plane(f * ROWS + k if f < 2 else 2 * ROWS + (f - 2) * MOMENTS + k)]

    def finish(self, dev):
        blocks = self.blocks
        lane = lax.broadcasted_iota(jnp.int32, (blocks, 128), 1)
        y = [self.rows_ref[self.plane(c)] for c in range(3)]
        score = jnp.zeros((blocks, 128), F32)
        total = [jnp.zeros((blocks, 128), F32)] * MOMENTS
        for f in range(5):
            v = self.rows_ref[self.plane(3 + f)]
            first = self.got(f, 0)
            self.part_ref[f, pl.ds(dev * blocks, blocks)] = first
            score = score + v * first
            v = v * (-2.0 * self.wide[f])
            total = [t + v * (first if k == 0 else self.got(f, k)) for k, t in enumerate(total)]
        index = [[4, 5, 6], [5, 7, 8], [6, 8, 9]]
        values = [score] + [total[1 + c] - y[c] * total[0] for c in range(3)]
        values += [total[index[c][d]] - y[c] * total[1 + d] for c in range(3) for d in range(3)]
        packed = jnp.zeros((blocks, 128), F32)
        for q, value in enumerate(values):
            packed = jnp.where(lane == q, jnp.sum(value, axis=1, keepdims=True), packed)
        flat = jnp.concatenate([packed, jnp.zeros((128 - blocks, 128), F32)], axis=0).T[:16]
        valid = slot_row(self.name_ref, dev, self.place) >= 0
        valid = jnp.concatenate([jnp.where(valid, 1.0, 0.0), jnp.zeros((1, 128 - blocks), F32)], axis=1)
        flat = jnp.where(valid > 0.0, flat, 0.0)
        out = flat[0:4]
        for q in range(1, 4):
            out = out + pltpu.roll(flat[4 * q:4 * q + 4], 32 * q, 1)
        return out

    def chunk(self, dev):
        self.atoms(dev)
        self.templates(dev)
        fronts, middles = {}, {}
        for n in range(-LEAD, 3 * self.blocks + LAG):
            u, e = divmod(n + LEAD, 3)
            if e == 0 and 0 <= u < self.blocks:
                fronts[u] = self.front(u)[1]
            u, e = divmod(n, 3)
            if 0 <= u < self.blocks:
                middles[n] = self.middle(u, fronts[u], e)
            if n >= LAG:
                self.back(*middles.pop(n - LAG))
        return self.finish(dev)

    @staticmethod
    def scratch(blocks):
        return [pltpu.VMEM((n * (blocks + 1), 128), F32) for n in (48, 8 * ROWS, 8, 24, 4 * ROWS)]


def main_kernel(libs, tmpls, xyz_ref, charge_ref, type_ref, chan_ref, owner_ref, slot_ref, points_hbm, weights_hbm, widths_hbm,
                table_hbm, part_hbm, got_ref, name_ref, real_ref, whole_ref, res_ref, points_ref, bf_ref, weights_ref, widths_ref, table_ref,
                part_ref, part_sem, local_sem,
                z_send, z_recv, x_send, x_recv, s_send, s_recv, r_send, r_recv, *scratch):
    l = lax.axis_index("lib")
    t = lax.axis_index("tmpl")
    s = lax.axis_index("sub")
    steps = libs * tmpls
    count = 2 * steps
    place = l * tmpls + t
    me = place * 2 + s
    blocks = real_ref.shape[2]
    half = blocks // 2
    moves = [(xyz_ref, real_ref.at[place, pl.ds(0, 3)]), (charge_ref, real_ref.at[place, 3]), (type_ref, whole_ref.at[place, 0]),
             (chan_ref, whole_ref.at[place, 1]), (owner_ref, name_ref.at[place, 0]), (slot_ref, name_ref.at[place, 1]),
             (widths_hbm, widths_ref), (table_hbm, table_ref), (points_hbm, points_ref), (weights_hbm, bf_ref)]
    moves = [pltpu.make_async_copy(src, dst, local_sem.at[n]) for n, (src, dst) in enumerate(moves)]
    for move in moves:
        move.start()
    barrier = pltpu.get_barrier_semaphore()

    @pl.loop(1, count)
    def _(k):
        other = lax.rem(me + k, count)
        where = {"lib": other // (2 * tmpls), "tmpl": lax.rem(other // 2, tmpls), "sub": lax.rem(other, 2)}
        pl.semaphore_signal(barrier, inc=1, device_id=where, device_id_type=MESH)

    for move in moves[:6]:
        move.wait()
    pl.semaphore_wait(barrier, count - 1)

    def lib_of(k, sign):
        if libs & (libs - 1):
            return lax.rem(l + sign * k + libs, libs)
        bits = [1 << b for b in range(libs.bit_length() - 1)]
        return sum((lax.rem(l // bit + k // bit, 2) * bit for bit in bits), jnp.int32(0))

    def owner_of(k, m):
        return lib_of(k, -1), lax.rem(t - m + tmpls, tmpls)

    def step_of(i):
        j = i // tmpls
        m = lax.rem(i, tmpls)
        return lib_step(j), m + ((j + 1) // libs) * (tmpls - 1 - 2 * m)

    def lib_step(j):
        return (lax.rem((2 - libs % 2) * (j + libs - 2), max(libs - 1, 1)) + 1) * ((j + libs - 1) // libs)

    def bundle(k, m, send, recv, device):
        lib, tmpl = owner_of(k, m)
        at = lib * tmpls + tmpl
        part = pl.ds(s * half, half)
        refs = (real_ref.at[at, :, part], whole_ref.at[at, :, part], name_ref.at[at, s])
        return [pltpu.make_async_remote_copy(src_ref=ref, dst_ref=ref, send_sem=send(n), recv_sem=recv(n), device_id=device,
                                             device_id_type=MESH) for n, ref in enumerate(refs)]

    def z_copy(k):
        return bundle(0, 0, lambda n: z_send.at[k, n], lambda n: z_recv.at[k, n], {"lib": lib_of(k, 1)})

    def x_copy(k, m):
        return bundle(k, 0, lambda n: x_send.at[k, m, n], lambda n: x_recv.at[k, m, n], {"tmpl": lax.rem(t + m, tmpls)})

    def s_copy(k, m):
        return bundle(k, m, lambda n: s_send.at[k, m, n], lambda n: s_recv.at[k, m, n], {"sub": 1 - s})

    def back_copy(i, c):
        lib, tmpl = owner_of(*step_of(i))
        where = {"lib": lib, "tmpl": tmpl, "sub": 1 - s} if c else {"lib": lib, "tmpl": tmpl}
        return pltpu.make_async_remote_copy(
            src_ref=res_ref.at[lib * tmpls + tmpl], dst_ref=got_ref.at[me], send_sem=r_send.at[i, c],
            recv_sem=r_recv.at[i, c], device_id=where, device_id_type=MESH)

    def part_copy(i):
        lib, tmpl = owner_of(*step_of(i))
        here = pl.ds((lib * tmpls + tmpl) * blocks, blocks)
        return pltpu.make_async_copy(part_ref.at[:, here], part_hbm.at[:, here], part_sem.at[i])

    def all_of(copies, act):
        for c in copies:
            getattr(c, act)()

    def z_pump(k):
        all_of(z_copy(k), "wait_recv")

        @pl.loop(1, tmpls)
        def _(m):
            all_of(x_copy(k, m), "start")

        all_of(s_copy(k, 0), "start")

    def x_pump(k, m):
        all_of(x_copy(k, m), "wait_recv")
        all_of(s_copy(k, m), "start")

    @pl.loop(1, tmpls)
    def _(m):
        all_of(x_copy(0, m), "start")

    @pl.loop(1, libs)
    def _(j):
        all_of(z_copy(lib_step(j)), "start")

    for move in moves[6:]:
        move.wait()

    pairs = Pairs(place, blocks, name_ref, widths_ref, table_ref, real_ref, whole_ref, points_ref, weights_ref, part_ref, *scratch)
    pairs.clear()

    @pl.loop(0, 5)
    def _(f):
        weights_ref[f] = bf_ref[f].astype(F32)

    mine = pltpu.make_async_copy(res_ref.at[place], got_ref.at[me], local_sem.at[10])

    @pl.loop(0, steps)
    def _(i):
        k, m = step_of(i)
        j = i // tmpls
        k1, m1 = step_of(i + 1)

        @pl.when((i > 0) & (lax.rem(i, tmpls) == 0) & (j + 1 < libs))
        def _():
            z_pump(lib_step(j + 1))

        @pl.when((i > 0) & (i + 1 < steps) & (m1 > 0))
        def _():
            x_pump(k1, m1)

        @pl.when(i > 0)
        def _():
            all_of(s_copy(k, m), "wait_recv")

        @pl.when(i == 1)
        def _():
            mine.start()

        @pl.when(i > 0)
        def _():
            back_copy(i - 1, 1).start()
            part_copy(i - 1).start()

        @pl.when(i > 1)
        def _():
            back_copy(i - 1, 0).start()

        lib, tmpl = owner_of(k, m)
        dev = lib * tmpls + tmpl
        res_ref[dev] = pairs.chunk(dev)

        @pl.when(i == 0)
        def _():
            if tmpls > 1:
                x_pump(0, 1)
            if libs > 1:
                z_pump(lib_step(1))

    mine.wait()

    @pl.loop(1, libs)
    def _(k):
        all_of(z_copy(k), "wait_send")
        all_of(s_copy(k, 0), "wait_send")

    @pl.loop(1, tmpls)
    def _(m):
        @pl.loop(0, libs)
        def _(k):
            all_of(x_copy(k, m), "wait_send")
            all_of(s_copy(k, m), "wait_send")

    back_copy(steps - 1, 1).start()
    back_copy(steps - 1, 0).start()
    part_copy(steps - 1).start()
    back_copy(0, 1).wait()

    @pl.loop(0, steps)
    def _(i):
        part_copy(i).wait()

    @pl.loop(1, steps)
    def _(i):
        for c in range(2):
            back_copy(i, c).wait()


def run(libs, tmpls, xyz, charge, types, chans, owners, slots, points, weights, widths, table):
    blocks = charge.shape[0]
    steps = libs * tmpls
    dma = pltpu.SemaphoreType.DMA
    vmem = pl.BlockSpec(memory_space=pltpu.VMEM)
    lead = (libs, tmpls)
    return pl.pallas_call(
        functools.partial(main_kernel, libs, tmpls),
        out_shape=(jax.ShapeDtypeStruct((5, steps * blocks, 128), F32), jax.ShapeDtypeStruct((2 * steps, 4, 128), F32),
                   jax.ShapeDtypeStruct((steps, 2) + owners.shape, jnp.int32)),
        in_specs=[pl.BlockSpec(memory_space=pl.ANY)] * 10,
        out_specs=(pl.BlockSpec(memory_space=pl.ANY), vmem, vmem),
        scratch_shapes=[pltpu.VMEM((steps, 4, blocks, 128), F32), pltpu.VMEM((steps, 2, blocks, 128), jnp.int32),
                        pltpu.VMEM((steps, 4, 128), F32), pltpu.VMEM(points.shape, F32), pltpu.VMEM(weights.shape, BF16),
                        pltpu.VMEM(weights.shape, F32), pltpu.SMEM(widths.shape, F32), pltpu.SMEM(table.shape, F32),
                        pltpu.VMEM((5, steps * blocks, 128), F32), dma((steps,)), dma((11,)), dma((libs, 3)), dma((libs, 3)), dma(lead + (3,)),
                        dma(lead + (3,)), dma(lead + (3,)), dma(lead + (3,)), dma((steps, 2)), dma((steps, 2))]
        + Pairs.scratch(blocks),
        compiler_params=pltpu.CompilerParams(collective_id=0, has_side_effects=True, vmem_limit_bytes=60 << 20),
    )(xyz, charge, types, chans, owners, slots, points, weights, widths, table)


def last_kernel(me, got_ref, owner_ref, name_ref, part_ref, score_ref, pose_ref, wg_ref):
    per_block, blocks = owner_ref.shape
    devices = name_ref.shape[0]
    owner = owner_ref[...]
    place = me()

    def add(o, carry):
        total, scores = carry
        both = got_ref[2 * o] + got_ref[2 * o + 1]
        scores = jnp.where(owner == o, jnp.broadcast_to(both[0:1, :blocks], (per_block, blocks)), scores)
        return total + both, scores

    zeros = (jnp.zeros((4, 128), F32), jnp.zeros((per_block, blocks), F32))
    total, scores = lax.fori_loop(0, got_ref.shape[0] // 2, add, zeros)
    score_ref[...] = scores
    rows = [total] + [pltpu.roll(total, 128 - 32 * q, 1) for q in range(1, 4)]
    pose_ref[...] = jnp.concatenate([rows[0][1:4], rows[1], rows[2], rows[3][0:1]], axis=0)[:, :blocks]
    tmpl_count = wg_ref.shape[1]
    step = math.gcd(devices, 8)
    tile = math.gcd(tmpl_count, 256)
    count = step * blocks

    def spread(g):
        rows = []
        for n in range(step):
            row = slot_row(name_ref, g * step + n, place)
            rows.append(row)
        slots = jnp.concatenate(rows, axis=1)
        parts = [part_ref[f, pl.ds(g * count, count)] for f in range(5)]
        halves = [split2(p) for p in parts]
        rhs = jnp.concatenate([jnp.concatenate([h[n] for h in halves], axis=1) for n in range(2)], axis=0)
        for r in range(0, tmpl_count, tile):
            here = lax.broadcasted_iota(jnp.int32, (tile, count), 0) + r
            pick = jnp.where(here == slots, 1.0, 0.0).astype(BF16)
            out = lax.dot_general(jnp.concatenate([pick, pick], axis=1), rhs, (((1,), (0,)), ((), ())), preferred_element_type=F32)
            yield r, out

    for r, out in spread(0):
        for f in range(5):
            wg_ref[f, pl.ds(r, tile)] = out[:, 128 * f:128 * f + 128]

    if devices > step:
        @pl.loop(1, devices // step)
        def _(g):
            for r, out in spread(g):
                for f in range(5):
                    wg_ref[f, pl.ds(r, tile)] += out[:, 128 * f:128 * f + 128]


def last(me, got, owner_rows, names, parts, tmpl_count):
    per_block, blocks = owner_rows.shape
    vmem = pl.BlockSpec(memory_space=pltpu.VMEM)
    return pl.pallas_call(
        functools.partial(last_kernel, me),
        out_shape=(jax.ShapeDtypeStruct((per_block, blocks), F32), jax.ShapeDtypeStruct((12, blocks), F32),
                   jax.ShapeDtypeStruct((5, tmpl_count, 128), F32)),
        in_specs=[vmem] * 4,
        out_specs=(vmem,) * 3,
        compiler_params=pltpu.CompilerParams(vmem_limit_bytes=60 << 20),
    )(got, owner_rows, names, parts)


def local(libs, tmpls, coords, atom_type, channel, charge, pair_owner, pair_slot, type_table, widths, tmpl_points,
          tmpl_weights):
    owners, slots = pair_owner.T, pair_slot.T

    def me():
        return lax.axis_index("lib") * tmpls + lax.axis_index("tmpl")

    parts, got, names = run(libs, tmpls, jnp.transpose(coords, (1, 0, 2)), charge, atom_type, channel, owners, slots,
                            jnp.transpose(tmpl_points, (1, 0, 2)), jnp.transpose(tmpl_weights, (1, 0, 2)), widths, type_table.T)
    scores, pose, weight_grad = last(me, got, owners, names, parts, tmpl_points.shape[0])
    return scores.T, pose.T, jnp.transpose(weight_grad, (1, 0, 2))


def solution(mesh):
    every = ("groups", "lib", "tmpl")
    in_specs = (P(every, None, None), P(every, None), P(every, None), P(every, None), P(every, None), P(every, None),
                P(), P(), P(("lib", "tmpl"), None, "sub"), P(("lib", "tmpl"), None, "sub"))
    out_specs = (P(every, None), P(every, None), P(every, None, "sub"))
    body = functools.partial(local, mesh.shape["lib"], mesh.shape["tmpl"])
    return jax.shard_map(body, mesh=mesh, in_specs=in_specs, out_specs=out_specs, check_vma=False)
```
